32 devices in a mesh: shard: 4 (over y, core), ctx: 8 (over z, x).
Axes of the slice: x: 2, y: 2, z: 4, core: 2. Of those that a mesh axis runs over, the one named last changes fastest.
Arguments:
- hidden_in: float32 [4, 2048, 640], P('shard', 'ctx'), may hold values from -50 to 50
- out_grad: float32 [4, 2048, 640], P('shard', 'ctx'), may hold values from -6 to 6
- seq_lengths: int32 [4, 4], P('shard'), may hold values from 1 to 1024, 2048 in all within a row
- block_deal: int32 [4, 16], P('shard'), may hold values from 0 to 15, each once within a row
- w_query: float32 [640, 1024], P('shard'), may hold values from -0.25 to 0.25
- w_key: float32 [640, 256], P('shard'), may hold values from -0.25 to 0.25
- w_value: float32 [640, 256], P('shard'), may hold values from -0.25 to 0.25
- w_output: float32 [1024, 640], P('shard'), may hold values from -0.1875 to 0.1875
- w_gate: float32 [640, 2048], P('shard'), may hold values from -0.25 to 0.25
- w_up: float32 [640, 2048], P('shard'), may hold values from -0.25 to 0.25
- w_down: float32 [2048, 640], P('shard'), may hold values from -0.125 to 0.125
- gain_input: float32 [640], replicated, may hold values from 0.5 to 1.5
- gain_query: float32 [256], replicated, may hold values from 0.5 to 1.5
- gain_key: float32 [256], replicated, may hold values from 0.5 to 1.5
- gain_post_attn: float32 [640], replicated, may hold values from 0.5 to 1.5
- gain_pre_ffn: float32 [640], replicated, may hold values from 0.5 to 1.5
- gain_post_ffn: float32 [640], replicated, may hold values from 0.5 to 1.5
- mom_query: float32 [640, 1024], P('shard'), may hold values from -217.2232 to 217.2232
- mom_key: float32 [640, 256], P('shard'), may hold values from -217.2232 to 217.2232
- mom_value: float32 [640, 256], P('shard'), may hold values from -217.2232 to 217.2232
- mom_output: float32 [1024, 640], P('shard'), may hold values from -217.2232 to 217.2232
- mom_gate: float32 [640, 2048], P('shard'), may hold values from -217.2232 to 217.2232
- mom_up: float32 [640, 2048], P('shard'), may hold values from -217.2232 to 217.2232
- mom_down: float32 [2048, 640], P('shard'), may hold values from -217.2232 to 217.2232
- gmom_input: float32 [640], replicated, may hold values from -217.2232 to 217.2232
- gmom_query: float32 [256], replicated, may hold values from -217.2232 to 217.2232
- gmom_key: float32 [256], replicated, may hold values from -217.2232 to 217.2232
- gmom_post_attn: float32 [640], replicated, may hold values from -217.2232 to 217.2232
- gmom_pre_ffn: float32 [640], replicated, may hold values from -217.2232 to 217.2232
- gmom_post_ffn: float32 [640], replicated, may hold values from -217.2232 to 217.2232
Outputs:
- block_out: float32 [4, 2048, 640], P('shard', 'ctx')
- input_grad: float32 [4, 2048, 640], P('shard', 'ctx')
- grad_query: float32 [640, 1024], P('shard')
- grad_key: float32 [640, 256], P('shard')
- grad_value: float32 [640, 256], P('shard')
- grad_output: float32 [1024, 640], P('shard')
- grad_gate: float32 [640, 2048], P('shard')
- grad_up: float32 [640, 2048], P('shard')
- grad_down: float32 [2048, 640], P('shard')
- grad_gain_input: float32 [640], replicated
- grad_gain_query: float32 [256], replicated
- grad_gain_key: float32 [256], replicated
- grad_gain_post_attn: float32 [640], replicated
- grad_gain_pre_ffn: float32 [640], replicated
- grad_gain_post_ffn: float32 [640], replicated
- new_query: float32 [640, 1024], P('shard')
- new_key: float32 [640, 256], P('shard')
- new_value: float32 [640, 256], P('shard')
- new_output: float32 [1024, 640], P('shard')
- new_gate: float32 [640, 2048], P('shard')
- new_up: float32 [640, 2048], P('shard')
- new_down: float32 [2048, 640], P('shard')
- new_mom_query: float32 [640, 1024], P('shard')
- new_mom_key: float32 [640, 256], P('shard')
- new_mom_value: float32 [640, 256], P('shard')
- new_mom_output: float32 [1024, 640], P('shard')
- new_mom_gate: float32 [640, 2048], P('shard')
- new_mom_up: float32 [640, 2048], P('shard')
- new_mom_down: float32 [2048, 640], P('shard')
- new_gain_input: float32 [640], replicated
- new_gain_query: float32 [256], replicated
- new_gain_key: float32 [256], replicated
- new_gain_post_attn: float32 [640], replicated
- new_gain_pre_ffn: float32 [640], replicated
- new_gain_post_ffn: float32 [640], replicated
- new_gmom_input: float32 [640], replicated
- new_gmom_query: float32 [256], replicated
- new_gmom_key: float32 [256], replicated
- new_gmom_post_attn: float32 [640], replicated
- new_gmom_pre_ffn: float32 [640], replicated
- new_gmom_post_ffn: float32 [640], replicated
The draws below stay inside these ranges and needn't reach their ends.
Inputs may be any that keep to these rules, and one draw needn't show every extreme that they name: `seq_lengths`: each row lists the lengths of a stream's sequences in order; they sum to 2048, and the longest is exactly 1024. `block_deal`: each row is a permutation of the stream's 16 blocks.
All inputs are finite; a program needn't handle non-finite values.
Results may differ from the reference program's by a relative error of at most 0.015.
The reference program's roundings to bfloat16 on the way count: a program that leaves them out, or rounds other values in their place, can miss the bound.
Values may be sent and summed in bfloat16 or wider, within the bound.
No kernel may reach another device: no remote copies, remote signals or barrier semaphores. Data moves between devices by JAX's collectives and lax.ppermute only.
A program may use at most 256 MiB of HBM per device.

```python
import math
import jax
import jax.numpy as jnp
import numpy as np
from jax import lax

D = 640
HEADS = 4
HEAD = 256
FF = 2048
BLK = 128
NS_ITERS = 5
QW = 1024
STREAMS = 4
CTX_TOK = 2048
NBLK = 16
SEQ_MAX = 1024
SEQS = 4


def draw_hidden_in(key, part):
    row_key, col_key, base_key = jax.random.split(key, 3)
    row_scale = jnp.exp((jax.random.uniform(row_key, (STREAMS, CTX_TOK, 1), jnp.float32) - 0.5) * math.log(10.0))
    col_scale = jnp.exp((jax.random.uniform(col_key, (1, 1, D), jnp.float32) - 0.5) * math.log(10.0))
    base = jnp.clip(jax.random.normal(base_key, (STREAMS, CTX_TOK, D), jnp.float32), -5.0, 5.0)
    return (base * row_scale * col_scale).astype(jnp.float32)


def levels(own_key, dims, pieces, least, top_value):
    def one(position, parts):
        heights = jax.random.uniform(jax.random.fold_in(jax.random.fold_in(own_key, 6), position), (parts,), jnp.float32, least / len(pieces), top_value / len(pieces))
        return jnp.repeat(jnp.exp(heights), dims[position] // parts).reshape((-1,) + (1,) * (len(dims) - position - 1))

    level = one(*pieces[0])
    for cut in pieces[1:]:
        level = level * one(*cut)
    return level


def length_profile(number_of, total, bound, skew):
    loads = [(1 << 20) // math.isqrt(grade ** skew) + 1 for grade in range(2, number_of + 1)]
    rest, holding = total - bound - (number_of - 1), [1] * (number_of - 1)
    while rest > 0:
        movable = [i for i in range(number_of - 1) if holding[i] < bound]
        pool, remaining = sum([loads[i] for i in movable]), rest
        for i in movable:
            addition = min(bound - holding[i], max(1, remaining * loads[i] // pool), rest)
            holding[i] = holding[i] + addition
            rest = rest - addition
    return np.array([bound] + holding)


def ragged(key, number_of, total, bound, slope):
    if number_of == 2:
        one = jax.random.randint(key, (), max(1, total - bound), min(bound, total - 1) + 1)
        return jnp.stack([one, total - one])
    tallies = jnp.asarray(length_profile(number_of, total, bound, slope), jnp.int32)
    twos = (number_of - 1) // 2
    giver, taker = tallies[1:1 + 2 * twos:2], tallies[2:2 + 2 * twos:2]
    slack = jnp.minimum(giver - 1, bound - taker)
    shifted = jax.random.randint(jax.random.fold_in(key, 1), (twos,), 0, 1 << 20) % (slack + 1)
    tallies = tallies.at[1:1 + 2 * twos:2].set(giver - shifted).at[2:2 + 2 * twos:2].set(taker + shifted)
    return tallies[jax.random.permutation(jax.random.fold_in(key, 2), number_of)]


def normal_values(stream_key, dims, deviation, most, pieces=(), held_as=jnp.bfloat16):
    drawn = deviation * jax.random.normal(stream_key, dims, jnp.float32)
    if pieces:
        drawn = drawn * levels(stream_key, dims, pieces, -0.22, 0.18)
    return jnp.clip(drawn, -most, most).astype(held_as)


def setup_inputs(seed: int = 0) -> dict:
    keys = jax.random.split(jax.random.key(seed), 31)
    hidden_in = draw_hidden_in(jax.random.fold_in(keys[30], 71), 0)
    out_grad = normal_values(keys[1], (STREAMS, CTX_TOK, D), 1.0, 6.0, ((0, 4), (1, 8)), jnp.float32)
    seq_lengths = jax.vmap(lambda own: ragged(own, SEQS, CTX_TOK, SEQ_MAX, 2))(jax.random.split(keys[2], STREAMS)).reshape((STREAMS, SEQS)).astype(jnp.int32)
    block_deal = jax.vmap(lambda own: jax.random.permutation(own, NBLK))(jax.random.split(keys[3], STREAMS)).reshape((STREAMS, NBLK)).astype(jnp.int32)
    w_query = normal_values(keys[4], (D, QW), D ** -0.5, 0.25, ((0, 4),), jnp.float32)
    w_key = normal_values(keys[5], (D, HEAD), D ** -0.5, 0.25, ((0, 4),), jnp.float32)
    w_value = normal_values(keys[6], (D, HEAD), D ** -0.5, 0.25, ((0, 4),), jnp.float32)
    w_output = normal_values(keys[7], (QW, D), QW ** -0.5, 0.1875, ((0, 4),), jnp.float32)
    w_gate = normal_values(keys[8], (D, FF), D ** -0.5, 0.25, ((0, 4),), jnp.float32)
    w_up = normal_values(keys[9], (D, FF), D ** -0.5, 0.25, ((0, 4),), jnp.float32)
    w_down = normal_values(keys[10], (FF, D), FF ** -0.5, 0.125, ((0, 4),), jnp.float32)
    gain_input = jnp.clip(1.0 + 0.1 * jax.random.normal(keys[11], (D,), jnp.float32), 0.5, 1.5)
    gain_query = jnp.clip(1.0 + 0.1 * jax.random.normal(keys[12], (HEAD,), jnp.float32), 0.5, 1.5)
    gain_key = jnp.clip(1.0 + 0.1 * jax.random.normal(keys[13], (HEAD,), jnp.float32), 0.5, 1.5)
    gain_post_attn = jnp.clip(1.0 + 0.1 * jax.random.normal(keys[14], (D,), jnp.float32), 0.5, 1.5)
    gain_pre_ffn = jnp.clip(1.0 + 0.1 * jax.random.normal(keys[15], (D,), jnp.float32), 0.5, 1.5)
    gain_post_ffn = jnp.clip(1.0 + 0.1 * jax.random.normal(keys[16], (D,), jnp.float32), 0.5, 1.5)
    mom_query = normal_values(keys[17], (D, QW), (0.4 * (STREAMS * CTX_TOK) ** 0.5), 217.2232, ((0, 4),), jnp.float32)
    mom_key = normal_values(keys[18], (D, HEAD), (0.4 * (STREAMS * CTX_TOK) ** 0.5), 217.2232, ((0, 4),), jnp.float32)
    mom_value = normal_values(keys[19], (D, HEAD), (0.4 * (STREAMS * CTX_TOK) ** 0.5), 217.2232, ((0, 4),), jnp.float32)
    mom_output = normal_values(keys[20], (QW, D), (0.4 * (STREAMS * CTX_TOK) ** 0.5), 217.2232, ((0, 4),), jnp.float32)
    mom_gate = normal_values(keys[21], (D, FF), (0.4 * (STREAMS * CTX_TOK) ** 0.5), 217.2232, ((0, 4),), jnp.float32)
    mom_up = normal_values(keys[22], (D, FF), (0.4 * (STREAMS * CTX_TOK) ** 0.5), 217.2232, ((0, 4),), jnp.float32)
    mom_down = normal_values(keys[23], (FF, D), (0.4 * (STREAMS * CTX_TOK) ** 0.5), 217.2232, ((0, 4),), jnp.float32)
    gmom_input = normal_values(keys[24], (D,), (0.4 * (STREAMS * CTX_TOK) ** 0.5), 217.2232, (), jnp.float32)
    gmom_query = normal_values(keys[25], (HEAD,), (0.4 * (STREAMS * CTX_TOK) ** 0.5), 217.2232, (), jnp.float32)
    gmom_key = normal_values(keys[26], (HEAD,), (0.4 * (STREAMS * CTX_TOK) ** 0.5), 217.2232, (), jnp.float32)
    gmom_post_attn = normal_values(keys[27], (D,), (0.4 * (STREAMS * CTX_TOK) ** 0.5), 217.2232, (), jnp.float32)
    gmom_pre_ffn = normal_values(keys[28], (D,), (0.4 * (STREAMS * CTX_TOK) ** 0.5), 217.2232, (), jnp.float32)
    gmom_post_ffn = normal_values(keys[29], (D,), (0.4 * (STREAMS * CTX_TOK) ** 0.5), 217.2232, (), jnp.float32)
    return dict(hidden_in=hidden_in, out_grad=out_grad, seq_lengths=seq_lengths, block_deal=block_deal, w_query=w_query, w_key=w_key, w_value=w_value, w_output=w_output, w_gate=w_gate, w_up=w_up, w_down=w_down, gain_input=gain_input, gain_query=gain_query, gain_key=gain_key, gain_post_attn=gain_post_attn, gain_pre_ffn=gain_pre_ffn, gain_post_ffn=gain_post_ffn, mom_query=mom_query, mom_key=mom_key, mom_value=mom_value, mom_output=mom_output, mom_gate=mom_gate, mom_up=mom_up, mom_down=mom_down, gmom_input=gmom_input, gmom_query=gmom_query, gmom_key=gmom_key, gmom_post_attn=gmom_post_attn, gmom_pre_ffn=gmom_pre_ffn, gmom_post_ffn=gmom_post_ffn)


EPSILON = 1e-06
ROPE_BASE = 1000000.0
SCORE_SCALE = 0.0625
MOMENTUM = 0.95
MATRIX_RATE = 0.04
GAIN_RATE = 0.1
COEF_A = 3.4445
COEF_B = -4.775
COEF_C = 2.0315
GELU_ROOT = math.sqrt(2.0 / math.pi)
GELU_CUBIC = 0.044715

def to_low(values):
    return lax.optimization_barrier(values.astype(jnp.bfloat16))

def norm_forward(values, gain_vec):
    inverse = lax.rsqrt(lax.optimization_barrier(jnp.mean(values * values, axis=-1, keepdims=True)) + EPSILON)
    normed = values * inverse
    return (normed * gain_vec, normed, inverse)

def norm_backward(upstream, normed, inverse, gain_vec):
    scaled = upstream * gain_vec
    grad_in = inverse * (scaled - normed * lax.optimization_barrier(jnp.mean(scaled * normed, axis=-1, keepdims=True)))
    gain_term = lax.optimization_barrier(jnp.sum((upstream * normed).reshape(-1, normed.shape[-1]), axis=0))
    return (grad_in, gain_term)

def gelu_parts(gate_lin):
    inner = GELU_ROOT * (gate_lin + GELU_CUBIC * gate_lin * gate_lin * gate_lin)
    tanh_val = jnp.tanh(inner)
    value_part = 0.5 * gate_lin * (1.0 + tanh_val)
    slope_part = 0.5 * (1.0 + tanh_val) + 0.5 * gate_lin * (1.0 - tanh_val * tanh_val) * GELU_ROOT * (1.0 + 3.0 * GELU_CUBIC * gate_lin * gate_lin)
    return (value_part, slope_part)

def rope_tables(positions, width):
    half_width = width // 2
    freq = jnp.exp(-(jnp.arange(half_width, dtype=jnp.float32) * (2.0 / width)) * math.log(ROPE_BASE))
    angles = positions.astype(jnp.float32)[:, None] * freq[None, :]
    return (jnp.cos(angles), jnp.sin(angles))

def rotate(values, cosine, sine):
    half_width = values.shape[-1] // 2
    first = values[..., :half_width]
    second = values[..., half_width:]
    return jnp.concatenate([first * cosine - second * sine, second * cosine + first * sine], axis=-1)

def rotate_back(grads, cosine, sine):
    half_width = grads.shape[-1] // 2
    first = grads[..., :half_width]
    second = grads[..., half_width:]
    return jnp.concatenate([first * cosine + second * sine, second * cosine - first * sine], axis=-1)

def token_layout(lengths_row, deal_row):
    offsets = jnp.arange(BLK, dtype=jnp.int32)
    stream_tok = (deal_row[:, None] * BLK + offsets[None, :]).reshape(-1).astype(jnp.int32)
    ends = jnp.cumsum(lengths_row, dtype=jnp.int32)
    passed = (stream_tok[:, None] >= ends[None, :]).astype(jnp.int32)
    segment = lax.optimization_barrier(jnp.sum(passed, axis=1, dtype=jnp.int32))
    positions = stream_tok - lax.optimization_barrier(jnp.sum(passed * lengths_row[None, :], axis=1, dtype=jnp.int32))
    return (segment, positions)

def newton_schulz(moment):
    tall_shape = moment.shape[0] > moment.shape[1]
    matrix = moment.T if tall_shape else moment
    current = to_low(matrix / (jnp.sqrt(jnp.sum(matrix * matrix)) + 1e-07))
    for iteration in range(NS_ITERS):
        gram = to_low(jnp.dot(current, current.T, preferred_element_type=jnp.float32))
        poly = to_low(COEF_B * gram.astype(jnp.float32) + COEF_C * jnp.dot(gram, gram, preferred_element_type=jnp.float32))
        current = to_low(COEF_A * current.astype(jnp.float32) + jnp.dot(poly, current, preferred_element_type=jnp.float32))
    result = current.astype(jnp.float32)
    return result.T if tall_shape else result

def attention_forward(query_rot, key_rot, value_low, segment, positions):
    row_count = query_rot.shape[0]
    head_count = query_rot.shape[1]
    query_block = math.gcd(row_count, 512)

    def one_block(block_index):
        start = block_index * query_block
        query_part = lax.dynamic_slice_in_dim(query_rot, start, query_block, 0)
        seg_part = lax.dynamic_slice_in_dim(segment, start, query_block, 0)
        pos_part = lax.dynamic_slice_in_dim(positions, start, query_block, 0)
        scores = jnp.einsum('qhd,kd->hqk', query_part.astype(jnp.float32), key_rot.astype(jnp.float32)) * SCORE_SCALE
        visible = (seg_part[:, None] == segment[None, :]) & (positions[None, :] <= pos_part[:, None])
        weights = jnp.where(visible[None], jnp.exp(scores), 0.0)
        totals = lax.optimization_barrier(jnp.sum(weights, axis=-1))
        summed = jnp.einsum('hqk,kd->qhd', to_low(weights).astype(jnp.float32), value_low.astype(jnp.float32))
        return (to_low(summed / totals.T[:, :, None]), jnp.log(totals))
    mixed, log_totals = lax.map(one_block, jnp.arange(row_count // query_block, dtype=jnp.int32))
    mixed = mixed.reshape(query_rot.shape)
    log_totals = jnp.transpose(log_totals, (1, 0, 2)).reshape(head_count, row_count)
    return (mixed, log_totals)

def attention_backward(query_rot, key_rot, value_low, mixed_grad_low, log_totals, delta, segment, positions):
    row_count = query_rot.shape[0]
    query_block = math.gcd(row_count, 512)

    def one_block(carry, block_index):
        key_acc, value_acc = carry
        start = block_index * query_block
        query_part = lax.dynamic_slice_in_dim(query_rot, start, query_block, 0)
        grad_part = lax.dynamic_slice_in_dim(mixed_grad_low, start, query_block, 0)
        seg_part = lax.dynamic_slice_in_dim(segment, start, query_block, 0)
        pos_part = lax.dynamic_slice_in_dim(positions, start, query_block, 0)
        lse_part = lax.dynamic_slice_in_dim(log_totals, start, query_block, 1)
        delta_part = lax.dynamic_slice_in_dim(delta, start, query_block, 1)
        scores = jnp.einsum('qhd,kd->hqk', query_part.astype(jnp.float32), key_rot.astype(jnp.float32)) * SCORE_SCALE
        visible = (seg_part[:, None] == segment[None, :]) & (positions[None, :] <= pos_part[:, None])
        probs = jnp.where(visible[None], jnp.exp(scores - lse_part[:, :, None]), 0.0)
        dprobs = jnp.einsum('qhd,kd->hqk', grad_part.astype(jnp.float32), value_low.astype(jnp.float32))
        score_grad = to_low(probs * (dprobs - delta_part[:, :, None]) * SCORE_SCALE).astype(jnp.float32)
        query_grad = jnp.einsum('hqk,kd->qhd', score_grad, key_rot.astype(jnp.float32))
        key_acc = key_acc + jnp.einsum('hqk,qhd->kd', score_grad, query_part.astype(jnp.float32))
        value_acc = value_acc + jnp.einsum('hqk,qhd->kd', to_low(probs).astype(jnp.float32), grad_part.astype(jnp.float32))
        return ((key_acc, value_acc), query_grad)
    zeros_kv = jnp.zeros((row_count, key_rot.shape[1]), jnp.float32)
    (key_grad, value_grad), query_grad = lax.scan(one_block, (zeros_kv, zeros_kv), jnp.arange(row_count // query_block, dtype=jnp.int32))
    return (query_grad.reshape(query_rot.shape), key_grad, value_grad)

def stream_pass(tokens, upstream, lengths_row, deal_row, lowered, gains):
    full_query, full_key, full_value, full_output, full_gate, full_up, full_down = lowered
    gain_input, gain_query, gain_key, gain_post_attn, gain_pre_ffn, gain_post_ffn = gains
    segment, positions = token_layout(lengths_row, deal_row)
    row_count = tokens.shape[0]
    cosine, sine = rope_tables(positions, HEAD)
    normed_in, base_in, inv_in = norm_forward(tokens, gain_input)
    attn_in = to_low(normed_in)
    query_lin = jnp.dot(attn_in, full_query, preferred_element_type=jnp.float32).reshape(row_count, HEADS, HEAD)
    key_lin = jnp.dot(attn_in, full_key, preferred_element_type=jnp.float32)
    value_lin = jnp.dot(attn_in, full_value, preferred_element_type=jnp.float32)
    query_normed, query_base, query_inv = norm_forward(query_lin, gain_query)
    key_normed, key_base, key_inv = norm_forward(key_lin, gain_key)
    query_rot = to_low(rotate(query_normed, cosine[:, None, :], sine[:, None, :]))
    key_rot = to_low(rotate(key_normed, cosine, sine))
    value_low = to_low(value_lin)
    mixed_low, log_totals = attention_forward(query_rot, key_rot, value_low, segment, positions)
    mixed_flat = mixed_low.reshape(row_count, HEADS * HEAD)
    attn_out = jnp.dot(mixed_flat, full_output, preferred_element_type=jnp.float32)
    post_attn, base_attn, inv_attn = norm_forward(attn_out, gain_post_attn)
    resid = tokens + post_attn
    normed_ffn, base_ffn, inv_ffn = norm_forward(resid, gain_pre_ffn)
    ffn_in = to_low(normed_ffn)
    gate_lin = jnp.dot(ffn_in, full_gate, preferred_element_type=jnp.float32)
    up_lin = jnp.dot(ffn_in, full_up, preferred_element_type=jnp.float32)
    gelu_value, gelu_slope = gelu_parts(gate_lin)
    hidden_low = to_low(gelu_value * up_lin)
    ffn_out = jnp.dot(hidden_low, full_down, preferred_element_type=jnp.float32)
    post_ffn, base_out, inv_out = norm_forward(ffn_out, gain_post_ffn)
    block_out = resid + post_ffn
    grad_ffn_out, term_post_ffn = norm_backward(upstream, base_out, inv_out, gain_post_ffn)
    ffn_grad_low = to_low(grad_ffn_out)
    grad_down = jnp.dot(hidden_low.T, ffn_grad_low, preferred_element_type=jnp.float32)
    grad_hidden = jnp.dot(ffn_grad_low, full_down.T, preferred_element_type=jnp.float32)
    gate_grad_low = to_low(grad_hidden * up_lin * gelu_slope)
    up_grad_low = to_low(grad_hidden * gelu_value)
    grad_gate = jnp.dot(ffn_in.T, gate_grad_low, preferred_element_type=jnp.float32)
    grad_up = jnp.dot(ffn_in.T, up_grad_low, preferred_element_type=jnp.float32)
    grad_ffn_in = jnp.dot(gate_grad_low, full_gate.T, preferred_element_type=jnp.float32) + jnp.dot(up_grad_low, full_up.T, preferred_element_type=jnp.float32)
    grad_resid_norm, term_pre_ffn = norm_backward(grad_ffn_in, base_ffn, inv_ffn, gain_pre_ffn)
    grad_resid = upstream + grad_resid_norm
    grad_attn_out, term_post_attn = norm_backward(grad_resid, base_attn, inv_attn, gain_post_attn)
    attn_grad_low = to_low(grad_attn_out)
    grad_output = jnp.dot(mixed_flat.T, attn_grad_low, preferred_element_type=jnp.float32)
    mixed_grad_low = to_low(jnp.dot(attn_grad_low, full_output.T, preferred_element_type=jnp.float32)).reshape(row_count, HEADS, HEAD)
    delta = lax.optimization_barrier(jnp.sum(mixed_grad_low.astype(jnp.float32) * mixed_low.astype(jnp.float32), axis=-1)).T
    grad_query_rot, grad_key_rot, grad_value_lin = attention_backward(query_rot, key_rot, value_low, mixed_grad_low, log_totals, delta, segment, positions)
    grad_query_normed = rotate_back(grad_query_rot, cosine[:, None, :], sine[:, None, :])
    grad_query_lin, term_query = norm_backward(grad_query_normed, query_base, query_inv, gain_query)
    grad_key_lin, term_key = norm_backward(rotate_back(grad_key_rot, cosine, sine), key_base, key_inv, gain_key)
    query_grad_low = to_low(grad_query_lin.reshape(row_count, HEADS * HEAD))
    key_grad_low = to_low(grad_key_lin)
    value_grad_low = to_low(grad_value_lin)
    grad_query = jnp.dot(attn_in.T, query_grad_low, preferred_element_type=jnp.float32)
    grad_key = jnp.dot(attn_in.T, key_grad_low, preferred_element_type=jnp.float32)
    grad_value = jnp.dot(attn_in.T, value_grad_low, preferred_element_type=jnp.float32)
    grad_attn_in = jnp.dot(query_grad_low, full_query.T, preferred_element_type=jnp.float32)
    grad_attn_in = grad_attn_in + jnp.dot(key_grad_low, full_key.T, preferred_element_type=jnp.float32)
    grad_attn_in = grad_attn_in + jnp.dot(value_grad_low, full_value.T, preferred_element_type=jnp.float32)
    grad_tokens_norm, term_input = norm_backward(grad_attn_in, base_in, inv_in, gain_input)
    input_grad = grad_resid + grad_tokens_norm
    weight_grads = (grad_query, grad_key, grad_value, grad_output, grad_gate, grad_up, grad_down)
    gain_grads = (term_input, term_query, term_key, term_post_attn, term_pre_ffn, term_post_ffn)
    return (block_out, input_grad, weight_grads, gain_grads)

def reference(hidden_in, out_grad, seq_lengths, block_deal, w_query, w_key, w_value, w_output, w_gate, w_up, w_down, gain_input, gain_query, gain_key, gain_post_attn, gain_pre_ffn, gain_post_ffn, mom_query, mom_key, mom_value, mom_output, mom_gate, mom_up, mom_down, gmom_input, gmom_query, gmom_key, gmom_post_attn, gmom_pre_ffn, gmom_post_ffn):
    masters = (w_query, w_key, w_value, w_output, w_gate, w_up, w_down)
    gains = (gain_input, gain_query, gain_key, gain_post_attn, gain_pre_ffn, gain_post_ffn)
    moments = (mom_query, mom_key, mom_value, mom_output, mom_gate, mom_up, mom_down)
    gain_moms = (gmom_input, gmom_query, gmom_key, gmom_post_attn, gmom_pre_ffn, gmom_post_ffn)
    lowered = tuple((to_low(matrix) for matrix in masters))

    def per_stream(carry, items):
        tokens, upstream, lengths_row, deal_row = items
        block_out, input_grad, weight_grads, gain_grads = stream_pass(tokens, upstream, lengths_row, deal_row, lowered, gains)
        weight_acc = tuple((first + second for first, second in zip(carry[0], weight_grads)))
        gain_acc = tuple((first + second for first, second in zip(carry[1], gain_grads)))
        return ((weight_acc, gain_acc), (block_out, input_grad))
    start_carry = (tuple((jnp.zeros(matrix.shape, jnp.float32) for matrix in masters)), tuple((jnp.zeros(vector.shape, jnp.float32) for vector in gains)))
    (weight_grads, gain_grads), (block_out, input_grad) = lax.scan(per_stream, start_carry, (hidden_in, out_grad, seq_lengths, block_deal))
    new_moms = tuple((MOMENTUM * moment + grad_term for moment, grad_term in zip(moments, weight_grads)))
    new_weights = []
    for matrix, moment in zip(masters, new_moms):
        ortho = newton_schulz(moment)
        factor = MATRIX_RATE * 0.2 * math.sqrt(max(matrix.shape[0], matrix.shape[1]))
        new_weights.append(matrix - factor * ortho)
    new_gmoms = tuple((MOMENTUM * moment + grad_term for moment, grad_term in zip(gain_moms, gain_grads)))
    new_gains = tuple((vector - GAIN_RATE * moment * lax.rsqrt(jnp.mean(moment * moment) + EPSILON) for vector, moment in zip(gains, new_gmoms)))
    return (block_out, input_grad, weight_grads[0], weight_grads[1], weight_grads[2], weight_grads[3], weight_grads[4], weight_grads[5], weight_grads[6], gain_grads[0], gain_grads[1], gain_grads[2], gain_grads[3], gain_grads[4], gain_grads[5], new_weights[0], new_weights[1], new_weights[2], new_weights[3], new_weights[4], new_weights[5], new_weights[6], new_moms[0], new_moms[1], new_moms[2], new_moms[3], new_moms[4], new_moms[5], new_moms[6], new_gains[0], new_gains[1], new_gains[2], new_gains[3], new_gains[4], new_gains[5], new_gmoms[0], new_gmoms[1], new_gmoms[2], new_gmoms[3], new_gmoms[4], new_gmoms[5])
```

```python
import math

import jax
import jax.numpy as jnp
from jax import lax
from jax.sharding import PartitionSpec as P

BLK = 128
NS_ITERS = 5
DEPTH = 4

EPSILON = 1e-06
ROPE_BASE = 1000000.0
SCORE_SCALE = 0.0625
MOMENTUM = 0.95
MATRIX_RATE = 0.04
GAIN_RATE = 0.1
COEF_A = 3.4445
COEF_B = -4.775
COEF_C = 2.0315
GELU_ROOT = math.sqrt(2.0 / math.pi)
GELU_CUBIC = 0.044715

BF = jnp.bfloat16
F32 = jnp.float32
BOTH = ("shard", "ctx")


def low(v):
    return v.astype(BF)


def dot(a, b, ca=1, cb=0):
    return lax.dot_general(a, b, (((ca,), (cb,)), ((), ())), preferred_element_type=F32)


def norm_forward(values, gain_vec):
    inverse = lax.rsqrt(jnp.mean(values * values, axis=-1, keepdims=True) + EPSILON)
    normed = values * inverse
    return (normed * gain_vec, normed, inverse)


def norm_backward(upstream, normed, inverse, gain_vec):
    scaled = upstream * gain_vec
    grad_in = inverse * (scaled - normed * jnp.mean(scaled * normed, axis=-1, keepdims=True))
    gain_term = jnp.sum(upstream * normed, axis=0)
    return (grad_in, gain_term)


def gelu_parts(gate_lin):
    inner = GELU_ROOT * (gate_lin + GELU_CUBIC * gate_lin * gate_lin * gate_lin)
    tanh_val = jnp.tanh(inner)
    value_part = 0.5 * gate_lin * (1.0 + tanh_val)
    slope_part = 0.5 * (1.0 + tanh_val) + 0.5 * gate_lin * (
        1.0 - tanh_val * tanh_val
    ) * GELU_ROOT * (1.0 + 3.0 * GELU_CUBIC * gate_lin * gate_lin)
    return (value_part, slope_part)


def rope_tables(positions, width):
    half_width = width // 2
    freq = jnp.exp(
        -(jnp.arange(half_width, dtype=F32) * (2.0 / width)) * math.log(ROPE_BASE)
    )
    angles = positions.astype(F32)[:, None] * freq[None, :]
    return (jnp.cos(angles), jnp.sin(angles))


def rotate(values, cosine, sine):
    half_width = values.shape[-1] // 2
    first = values[..., :half_width]
    second = values[..., half_width:]
    return jnp.concatenate(
        [first * cosine - second * sine, second * cosine + first * sine], axis=-1
    )


def rotate_back(grads, cosine, sine):
    half_width = grads.shape[-1] // 2
    first = grads[..., :half_width]
    second = grads[..., half_width:]
    return jnp.concatenate(
        [first * cosine + second * sine, second * cosine - first * sine], axis=-1
    )


def newton_schulz(moment):
    tall = moment.shape[0] > moment.shape[1]
    side = 0 if tall else 1
    current = low(moment / (jnp.sqrt(jnp.sum(moment * moment)) + 1e-07))
    for _ in range(NS_ITERS):
        gram = low(dot(current, current, side, side))
        poly = low(COEF_B * gram.astype(F32) + COEF_C * dot(gram, gram))
        moved = dot(current, poly, 1, 1) if tall else dot(poly, current)
        current = low(COEF_A * current.astype(F32) + moved)
    return current


def local(
    hidden_in,
    out_grad,
    seq_lengths,
    block_deal,
    w_query,
    w_key,
    w_value,
    w_output,
    w_gate,
    w_up,
    w_down,
    gain_input,
    gain_query,
    gain_key,
    gain_post_attn,
    gain_pre_ffn,
    gain_post_ffn,
    mom_query,
    mom_key,
    mom_value,
    mom_output,
    mom_gate,
    mom_up,
    mom_down,
    gmom_input,
    gmom_query,
    gmom_key,
    gmom_post_attn,
    gmom_pre_ffn,
    gmom_post_ffn,
):
    masters = (w_query, w_key, w_value, w_output, w_gate, w_up, w_down)
    gains = (gain_input, gain_query, gain_key, gain_post_attn, gain_pre_ffn, gain_post_ffn)
    moments = (mom_query, mom_key, mom_value, mom_output, mom_gate, mom_up, mom_down)
    gain_moms = (gmom_input, gmom_query, gmom_key, gmom_post_attn, gmom_pre_ffn, gmom_post_ffn)
    ctx_index = lax.axis_index("ctx")
    shard_index = lax.axis_index("shard")
    ctx_count = lax.axis_size("ctx")
    shard_count = lax.axis_size("shard")
    total = ctx_count * shard_count
    flat = shard_index * ctx_count + ctx_index
    wide = ctx_count // DEPTH

    core_bit = ctx_count
    y_bits = [ctx_count * 2 * (1 << i) for i in range((shard_count // 2).bit_length() - 1)]
    x_bits = [1 << i for i in range(wide.bit_length() - 1)]
    z_bits = [wide, 2 * wide]

    def swap(v, mask):
        return lax.ppermute(v, BOTH, [(i, i ^ mask) for i in range(total)])

    def bit_of(mask):
        return (flat // mask) % 2

    tokens = hidden_in[0]
    upstream = out_grad[0]
    rows, width = tokens.shape
    head = w_key.shape[1]
    qw = w_query.shape[1]
    heads = qw // head
    ff = w_gate.shape[1]

    def gather_rows(own):
        blocks = {0: own}
        for mask in y_bits + [core_bit]:
            blocks.update({off ^ mask: swap(v, mask) for off, v in list(blocks.items())})
        out = jnp.zeros((shard_count,) + own.shape, own.dtype)
        for off, v in blocks.items():
            where = shard_index ^ (off // ctx_count)
            out = lax.dynamic_update_slice(out, v[None], (where, 0, 0))
        return out.reshape(shard_count * own.shape[0], own.shape[1])

    full_kv = gather_rows(low(jnp.concatenate([w_key, w_value], axis=1)))
    full_q = gather_rows(low(w_query))
    full_o = gather_rows(low(w_output))
    full_gu = gather_rows(low(jnp.concatenate([w_gate, w_up], axis=1)))
    full_d = gather_rows(low(w_down))

    per_dev = block_deal.shape[1] // ctx_count
    deal = block_deal[0].reshape(ctx_count, per_dev)
    deal = deal[ctx_index ^ jnp.arange(ctx_count)]
    key_tok = (deal.reshape(-1)[:, None] * BLK + jnp.arange(BLK)[None, :]).reshape(-1)
    own_tok = key_tok[:rows]
    lengths = seq_lengths[0]
    ends = jnp.cumsum(lengths, dtype=jnp.int32)
    passed = (own_tok[:, None] >= ends[None, :]).astype(jnp.int32)
    own_start = jnp.sum(passed * lengths[None, :], axis=1, dtype=jnp.int32)
    cosine, sine = rope_tables(own_tok - own_start, head)

    normed_in, base_in, inv_in = norm_forward(tokens, gain_input)
    attn_in = low(normed_in)
    kv_lin = dot(attn_in, full_kv)
    key_normed, key_base, key_inv = norm_forward(kv_lin[:, :head], gain_key)
    key_value = jnp.concatenate(
        [low(rotate(key_normed, cosine, sine)), low(kv_lin[:, head:])], axis=1
    )

    kv_chunks = []
    for dz in range(DEPTH):
        part = key_value if dz == 0 else swap(key_value, dz * wide)
        for mask in x_bits:
            part = jnp.concatenate([part, swap(part, mask)], axis=0)
        kv_chunks.append(part)

    query_lin = dot(attn_in, full_q)
    q_state = []
    q_rot = []
    for h in range(heads):
        q_n, q_b, q_i = norm_forward(query_lin[:, h * head : (h + 1) * head], gain_query)
        q_state.append((q_b, q_i))
        q_rot.append(low(rotate(q_n, cosine, sine)))
    query = jnp.concatenate(q_rot, axis=0)

    def visible(dz):
        tok = key_tok[dz * wide * rows : (dz + 1) * wide * rows]
        return (tok[None, :] <= own_tok[:, None]) & (tok[None, :] >= own_start[:, None])

    totals = jnp.zeros((heads, rows, 1), F32)
    accum = jnp.zeros((heads * rows, head), F32)
    for dz in range(DEPTH):
        kv = kv_chunks[dz]
        scores = (dot(query, kv[:, :head], 1, 1) * SCORE_SCALE).reshape(heads, rows, -1)
        weights = jnp.where(visible(dz)[None], jnp.exp(scores), 0.0)
        totals = totals + jnp.sum(weights, axis=-1, keepdims=True)
        accum = accum + dot(low(weights).reshape(heads * rows, -1), kv[:, head:])
    log_totals = jnp.log(totals)
    mixed_h = low(accum / totals.reshape(heads * rows, 1))
    mixed = jnp.concatenate([mixed_h[h * rows : (h + 1) * rows] for h in range(heads)], axis=1)

    attn_out = dot(mixed, full_o)
    post_attn, base_attn, inv_attn = norm_forward(attn_out, gain_post_attn)
    resid = tokens + post_attn
    normed_ffn, base_ffn, inv_ffn = norm_forward(resid, gain_pre_ffn)
    ffn_in = low(normed_ffn)
    gu_lin = dot(ffn_in, full_gu)
    gate_lin, up_lin = gu_lin[:, :ff], gu_lin[:, ff:]
    gelu_value, gelu_slope = gelu_parts(gate_lin)
    hidden_low = low(gelu_value * up_lin)
    ffn_out = dot(hidden_low, full_d)
    post_ffn, base_out, inv_out = norm_forward(ffn_out, gain_post_ffn)
    block_out = resid + post_ffn

    def all_sum(partial, size, axis, order):
        def part(v, start, n):
            return lax.dynamic_slice_in_dim(v, start, n, axis)

        half = size // 2
        bit = bit_of(core_bit)
        got = swap(low(partial((1 - bit) * half, half)), core_bit)
        base = bit * half
        first = order[0]
        quarter = half // 2
        bit = bit_of(first)
        give = low(
            partial(base + (1 - bit) * quarter, quarter)
            + part(got, (1 - bit) * quarter, quarter).astype(F32)
        )
        keep = partial(base + bit * quarter, quarter) + part(
            got, bit * quarter, quarter
        ).astype(F32)
        cur = low(keep + swap(give, first).astype(F32))
        halved = [core_bit, first]
        n = quarter
        for mask in order[1:]:
            if n > 128:
                n //= 2
                bit = bit_of(mask)
                give = swap(part(cur, (1 - bit) * n, n), mask)
                cur = low(part(cur, bit * n, n).astype(F32) + give.astype(F32))
                halved.append(mask)
            else:
                cur = low(cur.astype(F32) + swap(cur, mask).astype(F32))
        for mask in reversed(halved):
            other = swap(cur, mask)
            bit = bit_of(mask)
            cur = jnp.concatenate(
                [jnp.where(bit == 0, cur, other), jnp.where(bit == 0, other, cur)], axis=axis
            )
        return cur

    order_y = y_bits + x_bits + z_bits
    order_x = x_bits + z_bits[:1] + y_bits + z_bits[1:]
    order_z = z_bits[:1] + y_bits + x_bits + z_bits[1:]

    grad_ffn_out, term_post_ffn = norm_backward(upstream, base_out, inv_out, gain_post_ffn)
    ffn_grad_low = low(grad_ffn_out)

    def columns(v, start, n):
        return lax.dynamic_slice_in_dim(v, start, n, 1)

    sum_down = all_sum(
        lambda a, n: dot(columns(hidden_low, a, n), ffn_grad_low, 0, 0), ff, 0, order_y
    )
    grad_hidden = dot(ffn_grad_low, full_d, 1, 1)
    gate_grad_low = low(grad_hidden * up_lin * gelu_slope)
    up_grad_low = low(grad_hidden * gelu_value)
    sum_gate = all_sum(
        lambda a, n: dot(ffn_in, columns(gate_grad_low, a, n), 0, 0), ff, 1, order_x
    )
    sum_up = all_sum(lambda a, n: dot(ffn_in, columns(up_grad_low, a, n), 0, 0), ff, 1, order_z)
    grad_ffn_in = dot(gate_grad_low, full_gu[:, :ff], 1, 1) + dot(
        up_grad_low, full_gu[:, ff:], 1, 1
    )
    grad_resid_norm, term_pre_ffn = norm_backward(grad_ffn_in, base_ffn, inv_ffn, gain_pre_ffn)
    grad_resid = upstream + grad_resid_norm
    grad_attn_out, term_post_attn = norm_backward(grad_resid, base_attn, inv_attn, gain_post_attn)
    attn_grad_low = low(grad_attn_out)
    sum_output = all_sum(
        lambda a, n: dot(columns(mixed, a, n), attn_grad_low, 0, 0), qw, 0, order_y
    )
    mixed_grad = low(dot(attn_grad_low, full_o, 1, 1))
    mixed_grad_h = jnp.concatenate(
        [mixed_grad[:, h * head : (h + 1) * head] for h in range(heads)], axis=0
    )
    delta = jnp.sum(
        mixed_grad_h.astype(F32) * mixed_h.astype(F32), axis=-1, keepdims=True
    ).reshape(heads, rows, 1)

    query_acc = jnp.zeros((heads * rows, head), F32)
    kv_grad = jnp.zeros((rows, 2 * head), F32)
    for dz in reversed(range(DEPTH)):
        kv = kv_chunks[dz]
        scores = (dot(query, kv[:, :head], 1, 1) * SCORE_SCALE).reshape(heads, rows, -1)
        probs = jnp.where(visible(dz)[None], jnp.exp(scores - log_totals), 0.0)
        dprobs = dot(mixed_grad_h, kv[:, head:], 1, 1).reshape(heads, rows, -1)
        score_grad = low(probs * (dprobs - delta) * SCORE_SCALE).reshape(heads * rows, -1)
        query_acc = query_acc + dot(score_grad, kv[:, :head])
        key_term = dot(score_grad, query, 0, 0)
        value_term = dot(low(probs).reshape(heads * rows, -1), mixed_grad_h, 0, 0)
        term = jnp.concatenate([key_term, value_term], axis=1)
        n = wide * rows
        for mask in reversed(x_bits):
            n //= 2
            term = term[:n] + swap(low(term[n:]), mask).astype(F32)
        if dz:
            term = swap(low(term), dz * wide).astype(F32)
        kv_grad = kv_grad + term

    q_grads = []
    term_query = jnp.zeros((head,), F32)
    for h in range(heads):
        back = rotate_back(query_acc[h * rows : (h + 1) * rows], cosine, sine)
        q_g, q_t = norm_backward(back, q_state[h][0], q_state[h][1], gain_query)
        q_grads.append(low(q_g))
        term_query = term_query + q_t
    query_grad_low = jnp.concatenate(q_grads, axis=1)
    sum_query = all_sum(
        lambda a, n: dot(attn_in, columns(query_grad_low, a, n), 0, 0), qw, 1, order_x
    )
    grad_key_lin, term_key = norm_backward(
        rotate_back(kv_grad[:, :head], cosine, sine), key_base, key_inv, gain_key
    )
    kv_grad_low = jnp.concatenate([low(grad_key_lin), low(kv_grad[:, head:])], axis=1)
    sum_kv = all_sum(
        lambda a, n: dot(attn_in, columns(kv_grad_low, a, n), 0, 0), 2 * head, 1, order_y
    )
    grad_attn_in = dot(query_grad_low, full_q, 1, 1) + dot(kv_grad_low, full_kv, 1, 1)
    grad_tokens_norm, term_input = norm_backward(grad_attn_in, base_in, inv_in, gain_input)
    input_grad = grad_resid + grad_tokens_norm

    terms = (term_input, term_query, term_key, term_post_attn, term_pre_ffn, term_post_ffn)
    packed = jnp.concatenate(terms).reshape(-1, 128)
    for mask in [core_bit] + order_y:
        packed = packed + swap(packed, mask)
    packed = packed.reshape(-1)
    gain_grads = []
    at = 0
    for t in terms:
        gain_grads.append(packed[at : at + t.shape[0]])
        at += t.shape[0]

    y_own = bit_of(y_bits[0])
    core = bit_of(core_bit)

    def flat_q(v):
        return v.reshape(-1, width)

    wide_own = [
        low(jnp.concatenate([mom_gate, mom_key], axis=1)),
        low(jnp.concatenate([mom_up, mom_value], axis=1)),
    ]
    long_own = [low(mom_down), low(jnp.concatenate([mom_output, flat_q(mom_query)], axis=0))]
    sets = [wide_own[0][None], wide_own[1][None], long_own[0][None], long_own[1][None]]
    for mask in y_bits[1:]:
        bit = bit_of(mask)
        grown = []
        for v in sets:
            other = swap(v, mask)
            grown.append(
                jnp.concatenate(
                    [jnp.where(bit == 0, v, other), jnp.where(bit == 0, other, v)], axis=0
                )
            )
        sets = grown
    pair = []
    for first, second in ((sets[0], sets[1]), (sets[2], sets[3])):
        mine = jnp.where(y_own == 0, first, second)
        got = swap(jnp.where(y_own == 0, second, first), y_bits[0])
        pair.append(
            jnp.stack(
                [jnp.where(y_own == 0, mine, got), jnp.where(y_own == 0, got, mine)], axis=1
            )
        )
    to_zero = [(i, i ^ core_bit) for i in range(total) if (i // core_bit) % 2 == 1]
    to_one = [(i, i ^ core_bit) for i in range(total) if (i // core_bit) % 2 == 0]
    got_wide = lax.ppermute(pair[0], BOTH, to_zero)
    got_long = lax.ppermute(pair[1], BOTH, to_one)
    mom_wide = jnp.stack([pair[0], got_wide], axis=2).reshape(width, -1)
    mom_long = jnp.stack([got_long, pair[1]], axis=2).reshape(shard_count, -1, width)

    out_rows = w_output.shape[0]

    def sharpen(mom_part, grad_part):
        return newton_schulz(MOMENTUM * mom_part.astype(F32) + grad_part.astype(F32))

    def own_gate(mw, ml, sg, su, sd, so, sq, skv):
        return (
            jnp.concatenate(
                [sharpen(mw[:, :ff], sg), sharpen(mw[:, ff:], skv[:, :head])], axis=1
            ),
            jnp.zeros_like(ml),
        )

    def own_up(mw, ml, sg, su, sd, so, sq, skv):
        return (
            jnp.concatenate(
                [sharpen(mw[:, :ff], su), sharpen(mw[:, ff:], skv[:, head:])], axis=1
            ),
            jnp.zeros_like(ml),
        )

    def own_down(mw, ml, sg, su, sd, so, sq, skv):
        return (jnp.zeros_like(mw), sharpen(ml.reshape(ff, width), sd).reshape(ml.shape))

    def own_rest(mw, ml, sg, su, sd, so, sq, skv):
        ortho_o = sharpen(ml[:, :out_rows].reshape(qw, width), so)
        ortho_q = sharpen(ml[:, out_rows:].reshape(width, qw), sq)
        return (
            jnp.zeros_like(mw),
            jnp.concatenate(
                [
                    ortho_o.reshape(shard_count, out_rows, width),
                    ortho_q.reshape(shard_count, out_rows, width),
                ],
                axis=1,
            ),
        )

    ortho_wide, ortho_long = lax.switch(
        y_own * 2 + core,
        (own_gate, own_down, own_up, own_rest),
        mom_wide,
        mom_long,
        sum_gate,
        sum_up,
        sum_down,
        sum_output,
        sum_query,
        sum_kv,
    )

    ortho_wide = ortho_wide.reshape(shard_count // 2, 2, -1, ortho_wide.shape[1])
    ortho_long = ortho_long.reshape(shard_count // 2, 2, -1, width)
    chip_row = shard_index // 2

    def spread(ortho, holder):
        mine = lax.dynamic_slice_in_dim(ortho, chip_row, 1, 0)[0]
        theirs = lax.dynamic_slice_in_dim(ortho, chip_row ^ 1, 1, 0)[0]
        across = [
            (i, i ^ y_bits[0]) for i in range(total) if (i // core_bit) % 2 == holder
        ]
        other = lax.ppermute(theirs, BOTH, across)
        both = jnp.stack(
            [jnp.where(y_own == 0, mine, other), jnp.where(y_own == 0, other, mine)]
        )
        sent = lax.ppermute(
            both[:, 1 - holder], BOTH, to_one if holder == 0 else to_zero
        )
        return jnp.where(core == holder, both[:, holder], sent)

    wide_rows = spread(ortho_wide, 0)
    long_rows = spread(ortho_long, 1)
    row_updates = (
        long_rows[1, out_rows:].reshape(w_query.shape),
        wide_rows[0, :, ff:],
        wide_rows[1, :, ff:],
        long_rows[1, :out_rows],
        wide_rows[0, :, :ff],
        wide_rows[1, :, :ff],
        long_rows[0],
    )

    def own_rows(v, like):
        return lax.dynamic_slice_in_dim(v, shard_index * like.shape[0], like.shape[0], 0)

    summed = (
        own_rows(sum_query, w_query).astype(F32),
        own_rows(sum_kv[:, :head], w_key).astype(F32),
        own_rows(sum_kv[:, head:], w_value).astype(F32),
        own_rows(sum_output, w_output).astype(F32),
        own_rows(sum_gate, w_gate).astype(F32),
        own_rows(sum_up, w_up).astype(F32),
        own_rows(sum_down, w_down).astype(F32),
    )
    new_moms = tuple(MOMENTUM * moment + term for moment, term in zip(moments, summed))
    new_weights = []
    for matrix, update in zip(masters, row_updates):
        most = max(matrix.shape[0] * shard_count, matrix.shape[1])
        factor = MATRIX_RATE * 0.2 * math.sqrt(most)
        new_weights.append(matrix - factor * update.astype(F32))
    new_gmoms = tuple(MOMENTUM * moment + term for moment, term in zip(gain_moms, gain_grads))
    new_gains = tuple(
        vector - GAIN_RATE * moment * lax.rsqrt(jnp.mean(moment * moment) + EPSILON)
        for vector, moment in zip(gains, new_gmoms)
    )
    return (
        block_out[None],
        input_grad[None],
        *summed,
        *gain_grads,
        *new_weights,
        *new_moms,
        *new_gains,
        *new_gmoms,
    )


def solution(mesh):
    stream = P("shard", "ctx", None)
    matrix = P("shard", None)
    return jax.shard_map(
        local,
        mesh=mesh,
        in_specs=(stream,) * 2 + (matrix,) * 9 + (P(),) * 6 + (matrix,) * 7 + (P(),) * 6,
        out_specs=(stream,) * 2 + (matrix,) * 7 + (P(),) * 6 + (matrix,) * 14 + (P(),) * 12,
        check_vma=False,
    )
```
